256 devices in a mesh: leaf: 32 (over z, x), sib: 8 (over y, core).
Axes of the slice: x: 4, y: 4, z: 8, core: 2. Of those that a mesh axis runs over, the one named last changes fastest.
Arguments:
- sources: float32 [131072, 128], P(('leaf', 'sib')), may hold values from -8 to 8
- ordering: int32 [131072], P(('leaf', 'sib')), may hold values from 0 to 131071, as said below
- diagonal_inverse: float32 [512, 256, 256], P(('leaf', 'sib')), as said below
- low_rank: float32 [131072, 128], P(('leaf', 'sib'))
- nearby_blocks: bfloat16 [512, 8, 256, 256], P(('leaf', 'sib')), may hold values from -0.125 to 0.125
- near_index: int32 [512, 8], P(('leaf', 'sib')), may hold values from 0 to 511, as said below
Outputs:
- solution: float32 [131072, 128], P(('leaf', 'sib'))
- coefficients: float32 [128, 128], replicated
The draws below stay inside these ranges and needn't reach their ends.
Inputs may be any that keep to these rules, and one draw needn't show every extreme that they name: `ordering`: each catalog row appears once, and the rows of leaf block i are i * 256 to i * 256 + 255. `near_index`: each entry names a leaf block other than its row's own, at most 2 blocks away from it; the distance 2 occurs. `diagonal_inverse`: each block is symmetric positive definite.
All inputs are finite; a program needn't handle non-finite values.
Results may differ from the reference program's by a relative error of at most 0.0034.
Values may be sent and summed in bfloat16 or wider, within the bound.
No kernel may reach another device: no remote copies, remote signals or barrier semaphores. Data moves between devices by JAX's collectives and lax.ppermute only.
A program may use at most 64 MiB of HBM per device.

```python
import math
import jax
import jax.numpy as jnp
from jax import lax

LEAF = 256
RHS = 128
FACTOR_RANK = 128
NEAR = 8
ITERS = 4
LEAF_DEV = 2
LEAVES = 512
POINTS = 131072


def ordering_values(key):
    keys = jax.random.split(key, LEAVES)
    shuffled = jax.vmap(lambda single: jax.random.permutation(single, LEAF))(keys)
    offsets = jnp.arange(LEAVES, dtype=jnp.int32)[:, None] * LEAF
    return (shuffled.astype(jnp.int32) + offsets).reshape(-1).astype(jnp.int32)


def factor_values(key):
    first_key, second_key = jax.random.split(jax.random.fold_in(key, 13), 2)
    position = jnp.arange(POINTS, dtype=jnp.float32) / POINTS
    profile = 1.0 + 2.0 * position
    rough = jnp.exp(jax.random.uniform(first_key, (POINTS,), jnp.float32, 0.0, math.log(10.0)))
    base = jax.random.normal(second_key, (POINTS, FACTOR_RANK), jnp.float32)
    scale = 0.15 / math.sqrt(POINTS)
    return (base * (profile * rough)[:, None] * scale).astype(jnp.float32)


def draw_ordering(key, part):
    return ordering_values(key)


def draw_low_rank(key, part):
    return factor_values(key)


def draw_sources(key, part):
    sign_key, noise_key = jax.random.split(jax.random.fold_in(key, 17))
    factor = factor_values(key)
    leaf_order = ordering_values(key)
    column_ids = jnp.arange(RHS, dtype=jnp.int32) % FACTOR_RANK
    shifted_ids = (jnp.arange(RHS, dtype=jnp.int32) + 3) % FACTOR_RANK
    signs = jax.random.randint(sign_key, (2, RHS), 0, 2).astype(jnp.float32) * 2.0 - 1.0
    flow = factor[:, column_ids] * signs[0][None, :] + 0.5 * factor[:, shifted_ids] * signs[1][None, :]
    flow = flow * (0.3 * math.sqrt(POINTS))
    catalog = jnp.zeros((POINTS, RHS), jnp.float32).at[leaf_order].set(flow)
    noise = jax.random.normal(noise_key, (POINTS, RHS), jnp.float32)
    return jnp.clip(catalog + noise, -8.0, 8.0).astype(jnp.float32)


def draw_near_index(key, part):
    first_key, second_key = jax.random.split(jax.random.fold_in(key, 7))
    distance = jax.random.randint(first_key, (LEAVES, NEAR), 1, LEAF_DEV + 1)
    direction = jax.random.randint(second_key, (LEAVES, NEAR), 0, 2) * 2 - 1
    row_ids = jnp.arange(LEAVES, dtype=jnp.int32)[:, None]
    target = row_ids + direction * distance
    outside = (target < 0) | (target >= LEAVES)
    target = jnp.where(outside, row_ids - direction * distance, target)
    target = target.at[0, 0].set(LEAF_DEV)
    return target.astype(jnp.int32)


def draw_diagonal_inverse(key, part):
    first_key, second_key = jax.random.split(jax.random.fold_in(key, 11))
    diagonal = jax.random.uniform(first_key, (LEAVES, LEAF), jnp.float32, 0.6, 1.0)
    noise = jax.random.normal(second_key, (LEAVES, LEAF, LEAF), jnp.float32)
    symmetric = (noise + jnp.swapaxes(noise, 1, 2)) * (0.12 / math.sqrt(LEAF))
    identity = jnp.eye(LEAF, dtype=jnp.float32)
    return (symmetric + identity[None, :, :] * diagonal[:, :, None]).astype(jnp.float32)


def block_scale(key, shape, cuts, smallest, top_value):
    factor_of = 1.0
    for dim, parts in cuts:
        draws = jax.random.uniform(jax.random.fold_in(jax.random.fold_in(key, 6), dim), (parts,), jnp.float32, smallest / len(cuts), top_value / len(cuts))
        factor_of = factor_of * jnp.repeat(jnp.exp(draws), shape[dim] // parts).reshape((-1,) + (1,) * (len(shape) - 1 - dim))
    return factor_of


def bell_draw(stream_key, extent, deviation, reach, shards=(), held_as=jnp.bfloat16):
    result = deviation * jax.random.normal(stream_key, extent, jnp.float32)
    if shards:
        result = result * block_scale(stream_key, extent, shards, -0.22, 0.18)
    return jnp.clip(result, -reach, reach).astype(held_as)


def setup_inputs(seed: int = 0) -> dict:
    seeds = jax.random.split(jax.random.key(seed), 7)
    sources = draw_sources(jax.random.fold_in(seeds[6], 71), 0)
    ordering = draw_ordering(jax.random.fold_in(seeds[6], 71), 0)
    diagonal_inverse = draw_diagonal_inverse(jax.random.fold_in(seeds[6], 71), 0)
    low_rank = draw_low_rank(jax.random.fold_in(seeds[6], 71), 0)
    nearby_blocks = bell_draw(seeds[4], (LEAVES, NEAR, LEAF, LEAF), (LEAF * NEAR) ** -0.5, 0.125, ((0, 256),))
    near_index = draw_near_index(jax.random.fold_in(seeds[6], 71), 0)
    return dict(sources=sources, ordering=ordering, diagonal_inverse=diagonal_inverse, low_rank=low_rank, nearby_blocks=nearby_blocks, near_index=near_index)


def reference(sources, ordering, diagonal_inverse, low_rank, nearby_blocks, near_index):
    highest_setting = lax.Precision.HIGHEST
    leaves = diagonal_inverse.shape[0]
    ordered_rows = sources[ordering].reshape(leaves, LEAF, RHS)
    block_list = low_rank.reshape(leaves, LEAF, FACTOR_RANK)
    lifted_vector = jnp.einsum('zym,zmw->zyw', diagonal_inverse, block_list, precision=highest_setting)
    core_matrix = jnp.eye(FACTOR_RANK, dtype=jnp.float32) + jnp.einsum('wju,wjp->up', block_list, lifted_vector, precision=highest_setting)
    triangle = jnp.linalg.cholesky(core_matrix)

    def apply_inverse(input_vector):
        scaled_rows = jnp.einsum('zym,zmw->zyw', diagonal_inverse, input_vector, precision=highest_setting)
        projected_rows = jnp.einsum('wju,wjp->up', block_list, scaled_rows, precision=highest_setting)
        coefficients = jax.scipy.linalg.cho_solve((triangle, True), projected_rows)
        result_vector = scaled_rows - jnp.einsum('eqb,bd->eqd', lifted_vector, coefficients, precision=highest_setting)
        return (result_vector, coefficients)
    iterate, coefficients = apply_inverse(ordered_rows)
    for sweep in range(ITERS):
        rounded = iterate.astype(jnp.bfloat16)

        def near_row(leaf_row):
            targets = near_index[leaf_row]
            piece_list = rounded[targets].astype(jnp.float32)
            return jnp.einsum('kab,kbr->ar', nearby_blocks[leaf_row].astype(jnp.float32), piece_list)
        image_vector = lax.map(near_row, jnp.arange(leaves, dtype=jnp.int32))
        iterate, coefficients = apply_inverse(ordered_rows - image_vector)
    return (iterate.reshape(leaves * LEAF, RHS), coefficients)
```

```python
import jax
import jax.numpy as jnp
from jax import lax
from jax.experimental import pallas as pl
from jax.experimental.pallas import tpu as pltpu
from jax.sharding import Mesh
from jax.sharding import PartitionSpec as P

ITERS = 4
LEVELS = ITERS + 1
AXES = ("leaf_0", "leaf_1", "sib_0", "sib_1")
PLANE = ("leaf_1", "sib_0", "sib_1")
LINE = "leaf_0"
F32 = jnp.float32
BF16 = jnp.bfloat16
VMEM_LIMIT = 16 * 1024 * 1024
VMEM = pl.BlockSpec(memory_space=pltpu.VMEM)
ANY = pl.BlockSpec(memory_space=pl.ANY)
HBM = pl.BlockSpec(memory_space=pltpu.HBM)
SMEM = pl.BlockSpec(memory_space=pltpu.SMEM)
TILE = 8
LANES = 128


def params():
    return pltpu.CompilerParams(vmem_limit_bytes=VMEM_LIMIT)


def dot(a, b):
    return jnp.dot(a, b, preferred_element_type=F32)


def dot_rows(a, b):
    return lax.dot_general(a, b, (((0,), (0,)), ((), ())), preferred_element_type=F32)


def exact_dot(a, b):
    return jnp.dot(a, b, preferred_element_type=F32, precision=lax.Precision.HIGHEST)


def parts(value):
    high = value.astype(BF16)
    return high, (value - high.astype(F32)).astype(BF16)


def dot3(a, b):
    (a_high, a_low), (b_high, b_low) = a, b
    return dot(a_high, b_high) + (dot(a_high, b_low) + dot(a_low, b_high))


def shape(dims, dtype=F32):
    return jax.ShapeDtypeStruct(dims, dtype)


def first_kernel(
    order_hbm, source_hbm, inverse_hbm, factor_hbm, near_hbm,
    basis_ref, sent_ref, high_ref, low_ref, near_ref, order_ref, source, factor, inverse, sems,
):
    leaves, size, _ = inverse.shape
    columns = source.shape[1]
    pairs = (
        (order_hbm, order_ref),
        (source_hbm, source),
        (factor_hbm, factor),
        (inverse_hbm, inverse),
        (near_hbm, near_ref),
    )
    copies = [pltpu.make_async_copy(a, b, sems.at[i]) for i, (a, b) in enumerate(pairs)]
    for copy in copies:
        copy.start()
    row = lax.broadcasted_iota(jnp.int32, (size, size), 0)
    copies[0].wait()
    copies[1].wait()
    ordered = []
    for leaf in range(leaves):
        here = pl.ds(leaf * size, size)
        order = order_ref[:, leaf * size : (leaf + 1) * size] & (size - 1)
        chosen = (row == order).astype(F32).astype(BF16)
        ordered.append(dot_rows(chosen, jnp.concatenate(parts(source[here, :]), axis=1)).astype(BF16))
    copies[2].wait()
    copies[3].wait()
    for leaf in range(leaves):
        here = pl.ds(leaf * size, size)
        factor_high, factor_low = parts(factor[here, :])
        inverse_high, inverse_low = parts(inverse[leaf])
        high_ref[leaf] = inverse_high
        low_ref[leaf] = inverse_low
        high = jnp.concatenate([ordered[leaf][:, :columns], factor_high], axis=1)
        low = jnp.concatenate([ordered[leaf][:, columns:], factor_low], axis=1)
        basis = dot3((inverse_high, inverse_low), (high, low))
        basis_ref[here, :] = basis
        sent_ref[here, :] = basis.astype(BF16)
    copies[4].wait()


def first_step(order, sources, inverse, factor, near):
    rows, columns = sources.shape
    width = columns + factor.shape[1]
    return pl.pallas_call(
        first_kernel,
        out_shape=(
            shape((rows, width)),
            shape((rows, width), BF16),
            shape(inverse.shape, BF16),
            shape(inverse.shape, BF16),
            shape(near.shape, BF16),
        ),
        in_specs=[HBM] * 5,
        out_specs=(VMEM,) * 5,
        scratch_shapes=[
            pltpu.VMEM(order.shape, jnp.int32),
            pltpu.VMEM(sources.shape, F32),
            pltpu.VMEM(factor.shape, F32),
            pltpu.VMEM(inverse.shape, F32),
            pltpu.SemaphoreType.DMA((5,)),
        ],
        compiler_params=params(),
        name="first_step",
    )(*(pltpu.with_memory_space_constraint(v, pltpu.HBM) for v in (order, sources, inverse, factor, near)))


def turn_kernel(factor_ref, basis_ref, high_ref, low_ref, sum_ref):
    factor_high, factor_low = parts(factor_ref[...])
    high_ref[...] = factor_high.T
    low_ref[...] = factor_low.T
    sum_ref[...] = dot3((high_ref[...], low_ref[...]), parts(basis_ref[...]))


def turned(factor, basis):
    rows, rank = factor.shape
    return pl.pallas_call(
        turn_kernel,
        out_shape=(shape((rank, rows), BF16), shape((rank, rows), BF16), shape((rank, basis.shape[1]))),
        compiler_params=params(),
        name="turned",
    )(factor, basis)


def project_kernel(high_ref, low_ref, value_ref, sum_ref):
    sum_ref[...] = dot3((high_ref[...], low_ref[...]), parts(value_ref[...]))


def projected(high, low, value):
    return pl.pallas_call(
        project_kernel,
        out_shape=shape((high.shape[0], value.shape[1])),
        compiler_params=params(),
        name="projected",
    )(high, low, value)


def sweep_kernel(
    target_ref, own_ref, pair_ref, cross_ref, near_ref, high_ref, low_ref, basis_ref, _,
    next_ref, sent_ref, window,
):
    leaves, near, size, _ = near_ref.shape
    for place, ref in enumerate((pair_ref, own_ref, cross_ref)):
        for leaf in range(leaves):
            window[place * leaves + leaf] = ref[leaf * size : (leaf + 1) * size, :]
    for leaf in range(leaves):
        here = pl.ds(leaf * size, size)
        image = dot(near_ref[leaf, 0], window[target_ref[leaf, 0]])
        for k in range(1, near):
            image += dot(near_ref[leaf, k], window[target_ref[leaf, k]])
        value = basis_ref[here, :] - dot3((high_ref[leaf], low_ref[leaf]), parts(image))
        next_ref[here, :] = value
        sent_ref[here, :] = value.astype(BF16)


def sweep(targets, own, pair, cross, near, high, low, basis, sums):
    leaves, size = near.shape[0], near.shape[2]
    return pl.pallas_call(
        sweep_kernel,
        out_shape=(shape(basis.shape), shape(basis.shape, BF16)),
        in_specs=[SMEM] + [VMEM] * 7 + [ANY],
        out_specs=(VMEM, VMEM),
        scratch_shapes=[pltpu.VMEM((3 * leaves, size, basis.shape[1]), BF16)],
        compiler_params=params(),
        name="sweep",
    )(targets, own, pair, cross, near, high, low, basis, sums)


def place_of(chunk, rank):
    half, rest = divmod(chunk * TILE, rank)
    return slice(rest, rest + TILE), slice(half * LANES, half * LANES + LANES)


def pack_kernel(high_ref, low_ref, value_ref, *refs):
    sum_refs, (out_ref, changes) = refs[:ITERS], refs[ITERS:]
    rank = changes.shape[1]
    sums = [ref[...] for ref in sum_refs]
    sums.append(dot3((high_ref[...], low_ref[...]), parts(value_ref[...])))
    start = sums[0].astype(BF16).astype(F32)
    changes[0] = start
    changes[1] = sums[0] - start
    for j in range(1, LEVELS):
        changes[j + 1] = sums[j] - sums[j - 1]
    for chunk in range(out_ref.shape[0]):
        rows, lanes = place_of(chunk, rank)
        for j in range(0, LEVELS + 1, 2):
            both = jnp.concatenate([changes[j, rows, lanes], changes[j + 1, rows, lanes]], axis=0)
            out_ref[chunk, j * TILE : (j + 2) * TILE, :] = both.astype(BF16)


def packed(high, low, value, sums, count):
    rank, width = sums[0].shape
    return pl.pallas_call(
        pack_kernel,
        out_shape=shape((count, (LEVELS + 1) * TILE, LANES), BF16),
        scratch_shapes=[pltpu.VMEM((LEVELS + 1, rank, width), F32)],
        compiler_params=params(),
        name="packed",
    )(high, low, value, *sums)


def add_kernel(in_ref, out_ref):
    total = in_ref[0].astype(F32)
    for i in range(1, in_ref.shape[0]):
        total += in_ref[i].astype(F32)
    total = jnp.concatenate([total[:TILE] + total[TILE : 2 * TILE], total[2 * TILE :]], axis=0)
    for i in range(out_ref.shape[0]):
        out_ref[i] = total


def added(arrived, count):
    return pl.pallas_call(
        add_kernel,
        out_shape=shape((count, arrived.shape[1] - TILE, LANES)),
        compiler_params=params(),
        name="added",
    )(arrived)


def split_kernel(in_ref, out_ref):
    total = in_ref[0]
    for i in range(1, in_ref.shape[0]):
        total += in_ref[i]
    start = total[:TILE].astype(BF16).astype(F32)
    total = jnp.concatenate([start, total[:TILE] - start, total[TILE:]], axis=0).astype(BF16)
    for i in range(out_ref.shape[0]):
        out_ref[i] = total


def split(arrived, count):
    return pl.pallas_call(
        split_kernel,
        out_shape=shape((count, arrived.shape[1] + TILE, LANES), BF16),
        compiler_params=params(),
        name="split",
    )(arrived)


def inverse_of(core, eye):
    diagonal = 1.0 / jnp.sum(core * eye, axis=0, keepdims=True)
    size = jnp.max(jnp.sum(jnp.abs(core), axis=0))
    spread = jnp.max(jnp.sum(jnp.abs(eye - core * diagonal), axis=0))
    scale = jnp.where(spread < 0.9, diagonal, 2.0 / (1.0 + size))

    def keep_going(state):
        step, _, rest = state
        return jnp.logical_and(step < 48, jnp.max(jnp.abs(rest)) > 1e-6)

    def improve(state):
        step, value, rest = state
        value = value + exact_dot(value, rest)
        return step + 1, value, eye - exact_dot(core, value)

    return lax.while_loop(keep_going, improve, (0, eye * scale, eye - core * scale))[1]


def last_kernel(arrived_ref, *refs):
    basis_refs, (solution_ref, coefficients_ref, total) = refs[:LEVELS], refs[LEVELS:]
    rank = total.shape[1]
    columns = total.shape[2] - rank
    for chunk in range(arrived_ref.shape[0]):
        rows, lanes = place_of(chunk, rank)
        for j in range(0, LEVELS + 1, 2):
            both = arrived_ref[chunk, j * TILE : (j + 2) * TILE, :].astype(F32)
            if j == 0:
                total[0, rows, lanes] = both[:TILE] + both[TILE:]
            else:
                total[j - 1, rows, lanes] = both[:TILE]
                total[j, rows, lanes] = both[TILE:]
    eye = (
        lax.broadcasted_iota(jnp.int32, (rank, rank), 0) == lax.broadcasted_iota(jnp.int32, (rank, rank), 1)
    ).astype(F32)
    core_inverse = parts(inverse_of(eye + total[0, :, columns:], eye))
    change = [None] + [parts(dot3(core_inverse, parts(total[j, :, columns:]))) for j in range(1, LEVELS)]
    right = total[0, :, :columns]
    plain = [dot3(core_inverse, parts(right))]
    for k in range(1, LEVELS):
        right += total[k, :, :columns]
        plain.append(dot3(core_inverse, parts(right)))
    found, halves = [], []
    for k in range(LEVELS):
        value = plain[k]
        for j in range(k, 0, -1):
            value -= dot3(change[j], halves[k - j])
        found.append(value)
        halves.append(parts(value))
    coefficients_ref[...] = found[-1]
    solution = basis_refs[-1][:, :columns]
    for k in range(LEVELS):
        weight = found[ITERS - k]
        if k < ITERS:
            weight = weight - found[ITERS - k - 1]
        solution -= dot3(parts(basis_refs[k][:, columns:]), parts(weight))
    solution_ref[...] = solution


def last_step(arrived, bases, rank):
    rows, width = bases[0].shape
    return pl.pallas_call(
        last_kernel,
        out_shape=(shape((rows, width - rank)), shape((rank, width - rank))),
        scratch_shapes=[pltpu.VMEM((LEVELS, rank, width), F32)],
        compiler_params=params(),
        name="last_step",
    )(arrived, *bases)


def exchanged(array, axes):
    return lax.all_to_all(array, axes, 0, 0, tiled=True)


def on_device(sources, ordering, inverse, low_rank, nearby_blocks, near_index):
    leaves = inverse.shape[0]
    count = lax.axis_size(AXES)
    position = lax.axis_index(AXES)
    even = position % 2 == 0
    offset = near_index - position * leaves
    after = 2 * leaves
    targets = jnp.where(
        offset < 0,
        offset + leaves + jnp.where(even, after, 0),
        jnp.where(offset < leaves, offset + leaves, offset - leaves + jnp.where(even, 0, after)),
    )
    within = [(i, i ^ 1) for i in range(count)]
    across = [(i, j) for i in range(1, count - 1) for j in (i + 1 if i % 2 else i - 1,)]
    basis, sent, inverse_high, inverse_low, near = first_step(
        ordering.reshape(1, -1), sources, inverse, low_rank, nearby_blocks
    )
    bases, sums = [basis], []
    for k in range(ITERS):
        cross = lax.ppermute(sent, AXES, across)
        pair = lax.ppermute(sent, AXES, within)
        if k == 0:
            high, low, latest = turned(low_rank, basis)
        else:
            latest = projected(high, low, bases[-1])
        sums.append(latest)
        value, sent = sweep(targets, sent, pair, cross, near, inverse_high, inverse_low, basis, latest)
        bases.append(value)
    plane, line = lax.axis_size(PLANE), lax.axis_size(LINE)
    arrived = exchanged(packed(high, low, bases[-1], sums, plane), PLANE)
    arrived = exchanged(added(arrived, line), LINE)
    arrived = exchanged(split(arrived, plane), PLANE)
    return last_step(arrived, bases, low_rank.shape[1])


def solution(mesh):
    torus = Mesh(mesh.devices.reshape(8, 4, 4, 2), AXES)
    placed = (
        P(AXES, None),
        P(AXES),
        P(AXES, None, None),
        P(AXES, None),
        P(AXES, None, None, None),
        P(AXES, None),
    )
    return jax.shard_map(
        on_device, mesh=torus, in_specs=placed, out_specs=(P(AXES, None), P()), check_vma=False
    )
```

```python
import functools

import jax
import jax.numpy as jnp
from jax import lax
from jax.experimental import pallas as pl
from jax.experimental.pallas import tpu as pltpu
from jax.sharding import Mesh
from jax.sharding import PartitionSpec as P

ITERS = 4
LEVELS = ITERS + 1
AXES = ("leaf_0", "leaf_1", "sib_0", "sib_1")
PLANE = ("leaf_1", "sib_0", "sib_1")
LINE = "leaf_0"
F32 = jnp.float32
BF16 = jnp.bfloat16
VMEM_LIMIT = 16 * 1024 * 1024
VMEM = pl.BlockSpec(memory_space=pltpu.VMEM)
ANY = pl.BlockSpec(memory_space=pl.ANY)
HBM = pl.BlockSpec(memory_space=pltpu.HBM)
SMEM = pl.BlockSpec(memory_space=pltpu.SMEM)
TILE = 8
LANES = 128


def params():
    return pltpu.CompilerParams(vmem_limit_bytes=VMEM_LIMIT)


def dot(a, b):
    return jnp.dot(a, b, preferred_element_type=F32)


def dot_rows(a, b):
    return lax.dot_general(a, b, (((0,), (0,)), ((), ())), preferred_element_type=F32)


def exact_dot(a, b):
    return jnp.dot(a, b, preferred_element_type=F32, precision=lax.Precision.HIGHEST)


def parts(value):
    high = value.astype(BF16)
    return high, (value - high.astype(F32)).astype(BF16)


def dot3(a, b):
    (a_high, a_low), (b_high, b_low) = a, b
    return dot(a_high, b_high) + (dot(a_high, b_low) + dot(a_low, b_high))


def shape(dims, dtype=F32):
    return jax.ShapeDtypeStruct(dims, dtype)


def first_kernel(
    order_hbm, source_hbm, inverse_hbm, factor_hbm, near_hbm,
    basis_ref, sent_ref, high_ref, low_ref, near_ref, order_ref, source, factor, inverse, sems,
):
    leaves, size, _ = inverse.shape
    columns = source.shape[1]
    pairs = (
        (order_hbm, order_ref),
        (source_hbm, source),
        (factor_hbm, factor),
        (inverse_hbm, inverse),
        (near_hbm, near_ref),
    )
    copies = [pltpu.make_async_copy(a, b, sems.at[i]) for i, (a, b) in enumerate(pairs)]
    for copy in copies:
        copy.start()
    row = lax.broadcasted_iota(jnp.int32, (size, size), 0)
    copies[0].wait()
    copies[1].wait()
    ordered = []
    for leaf in range(leaves):
        here = pl.ds(leaf * size, size)
        order = order_ref[:, leaf * size : (leaf + 1) * size] & (size - 1)
        chosen = (row == order).astype(F32).astype(BF16)
        ordered.append(dot_rows(chosen, jnp.concatenate(parts(source[here, :]), axis=1)).astype(BF16))
    copies[2].wait()
    copies[3].wait()
    for leaf in range(leaves):
        here = pl.ds(leaf * size, size)
        factor_high, factor_low = parts(factor[here, :])
        inverse_high, inverse_low = parts(inverse[leaf])
        high_ref[leaf] = inverse_high
        low_ref[leaf] = inverse_low
        high = jnp.concatenate([ordered[leaf][:, :columns], factor_high], axis=1)
        low = jnp.concatenate([ordered[leaf][:, columns:], factor_low], axis=1)
        basis = dot3((inverse_high, inverse_low), (high, low))
        basis_ref[here, :] = basis
        sent_ref[here, :] = basis.astype(BF16)
    copies[4].wait()


def first_step(order, sources, inverse, factor, near):
    rows, columns = sources.shape
    width = columns + factor.shape[1]
    return pl.pallas_call(
        first_kernel,
        out_shape=(
            shape((rows, width)),
            shape((rows, width), BF16),
            shape(inverse.shape, BF16),
            shape(inverse.shape, BF16),
            shape(near.shape, BF16),
        ),
        in_specs=[HBM] * 5,
        out_specs=(VMEM,) * 5,
        scratch_shapes=[
            pltpu.VMEM(order.shape, jnp.int32),
            pltpu.VMEM(sources.shape, F32),
            pltpu.VMEM(factor.shape, F32),
            pltpu.VMEM(inverse.shape, F32),
            pltpu.SemaphoreType.DMA((5,)),
        ],
        compiler_params=params(),
        name="first_step",
    )(*(pltpu.with_memory_space_constraint(v, pltpu.HBM) for v in (order, sources, inverse, factor, near)))


def turn_kernel(
    target_ref, factor_ref, basis_ref, near_ref,
    high_ref, low_ref, sum_ref, own_ref, pair_ref, cross_ref, total,
):
    leaves, near, size, _ = near_ref.shape
    columns = basis_ref.shape[1] - factor_ref.shape[1]
    rank = factor_ref.shape[1]
    factor_high, factor_low = parts(factor_ref[...])
    high_ref[...] = factor_high.T
    low_ref[...] = factor_low.T
    sum_ref[...] = dot3((high_ref[...], low_ref[...]), parts(basis_ref[...]))
    total[...] = jnp.zeros_like(total)
    for leaf in range(leaves):
        lifted = basis_ref[leaf * size : (leaf + 1) * size, columns:].astype(BF16).T
        for k in range(near):
            total[target_ref[leaf, k]] += dot(lifted, near_ref[leaf, k])
    for leaf in range(leaves):
        here = slice(leaf * rank, (leaf + 1) * rank)
        pair_ref[here, :] = total[leaf].astype(BF16)
        own_ref[here, :] = total[leaves + leaf]
        cross_ref[here, :] = total[2 * leaves + leaf].astype(BF16)


def turned(targets, factor, basis, near):
    rows, rank = factor.shape
    leaves, size = near.shape[0], near.shape[2]
    back = (leaves * rank, size)
    return pl.pallas_call(
        turn_kernel,
        out_shape=(
            shape((rank, rows), BF16),
            shape((rank, rows), BF16),
            shape((rank, basis.shape[1])),
            shape(back),
            shape(back, BF16),
            shape(back, BF16),
        ),
        in_specs=[SMEM] + [VMEM] * 3,
        out_specs=(VMEM,) * 6,
        scratch_shapes=[pltpu.VMEM((3 * leaves, rank, size), F32)],
        compiler_params=params(),
        name="turned",
    )(targets, factor, basis, near)


def project_kernel(high_ref, low_ref, value_ref, sum_ref):
    sum_ref[...] = dot3((high_ref[...], low_ref[...]), parts(value_ref[...]))


def projected(high, low, value):
    return pl.pallas_call(
        project_kernel,
        out_shape=shape((high.shape[0], value.shape[1])),
        compiler_params=params(),
        name="projected",
    )(high, low, value)


def last_sweep_kernel(arrived_ref, *refs):
    added_ref, window = refs[-2], refs[-1]
    sweep_kernel(0, *refs[:8], None, refs[8], window)
    total = arrived_ref[0].astype(F32)
    for i in range(1, arrived_ref.shape[0]):
        total += arrived_ref[i].astype(F32)
    total = jnp.concatenate([total[:TILE] + total[TILE : 2 * TILE], total[2 * TILE :]], axis=0)
    for i in range(added_ref.shape[0]):
        added_ref[i] = total


def last_sweep(arrived, count, targets, own, pair, cross, near, high, low, basis):
    leaves, size = near.shape[0], near.shape[2]
    return pl.pallas_call(
        last_sweep_kernel,
        out_shape=(shape(basis.shape), shape((count, arrived.shape[1] - TILE, LANES))),
        in_specs=[VMEM, SMEM] + [VMEM] * 7,
        out_specs=(VMEM, VMEM),
        scratch_shapes=[pltpu.VMEM((3 * leaves, size, basis.shape[1]), BF16)],
        compiler_params=params(),
        name="last_sweep",
    )(arrived, targets, own, pair, cross, near, high, low, basis)


def sweep_kernel(extras, target_ref, own_ref, pair_ref, cross_ref, near_ref, high_ref, low_ref, basis_ref, *refs):
    extra_refs, next_ref, sent_refs, window = refs[1 : 1 + extras], refs[1 + extras], refs[2 + extras : -1], refs[-1]
    leaves, near, size, _ = near_ref.shape
    for place, ref in enumerate((pair_ref, own_ref, cross_ref)):
        for leaf in range(leaves):
            window[place * leaves + leaf] = ref[leaf * size : (leaf + 1) * size, :]
    for extra_ref, sent_ref in zip(extra_refs, sent_refs):
        sent_ref[leaves * size :, :] = extra_ref[...]
    for leaf in range(leaves):
        here = pl.ds(leaf * size, size)
        image = dot(near_ref[leaf, 0], window[target_ref[leaf, 0]])
        for k in range(1, near):
            image += dot(near_ref[leaf, k], window[target_ref[leaf, k]])
        value = basis_ref[here, :] - dot3((high_ref[leaf], low_ref[leaf]), parts(image))
        next_ref[here, :] = value
        for sent_ref in sent_refs:
            sent_ref[here, :] = value.astype(BF16)


def sweep(targets, own, pair, cross, near, high, low, basis, after, extras, sends):
    leaves, size = near.shape[0], near.shape[2]
    rows, width = basis.shape
    sent = shape((rows + (extras[0].shape[0] if extras else 0), width), BF16)
    return pl.pallas_call(
        functools.partial(sweep_kernel, len(extras)),
        out_shape=(shape(basis.shape),) + (sent,) * sends,
        in_specs=[SMEM] + [VMEM] * 7 + [ANY] + [VMEM] * len(extras),
        out_specs=(VMEM,) * (1 + sends),
        scratch_shapes=[pltpu.VMEM((3 * leaves, size, width), BF16)],
        compiler_params=params(),
        name="sweep",
    )(targets, own, pair, cross, near, high, low, basis, after, *extras)


def place_of(chunk, rank):
    half, rest = divmod(chunk * TILE, rank)
    return slice(rest, rest + TILE), slice(half * LANES, half * LANES + LANES)


def pack_kernel(high_ref, low_ref, value_ref, sent_ref, own_ref, pair_ref, cross_ref, *refs):
    sum_refs, (out_ref, changes) = refs[: ITERS - 1], refs[ITERS - 1 :]
    rank = changes.shape[1]
    size = own_ref.shape[1]
    leaves = own_ref.shape[0] // rank
    sums = [ref[...] for ref in sum_refs]
    sums.append(dot3((high_ref[...], low_ref[...]), parts(value_ref[...])))
    final = sums[0]
    for leaf in range(leaves):
        here = slice(leaf * rank, (leaf + 1) * rank)
        there = slice(leaves * size + leaf * rank, leaves * size + (leaf + 1) * rank)
        back_high, back_low = parts(own_ref[here, :] + pair_ref[there, :].astype(F32) + cross_ref[there, :].astype(F32))
        sent = sent_ref[leaf * size : (leaf + 1) * size, :]
        final -= dot(back_high, sent) + dot(back_low, sent)
    sums.append(final)
    start = sums[0].astype(BF16).astype(F32)
    changes[0] = start
    changes[1] = sums[0] - start
    for j in range(1, LEVELS):
        changes[j + 1] = sums[j] - sums[j - 1]
    for chunk in range(out_ref.shape[0]):
        rows, lanes = place_of(chunk, rank)
        for j in range(0, LEVELS + 1, 2):
            both = jnp.concatenate([changes[j, rows, lanes], changes[j + 1, rows, lanes]], axis=0)
            out_ref[chunk, j * TILE : (j + 2) * TILE, :] = both.astype(BF16)


def packed(high, low, value, sent, back, sums, count):
    rank, width = sums[0].shape
    return pl.pallas_call(
        pack_kernel,
        out_shape=shape((count, (LEVELS + 1) * TILE, LANES), BF16),
        scratch_shapes=[pltpu.VMEM((LEVELS + 1, rank, width), F32)],
        compiler_params=params(),
        name="packed",
    )(high, low, value, sent, *back, *sums)


def split_kernel(in_ref, out_ref):
    total = in_ref[0]
    for i in range(1, in_ref.shape[0]):
        total += in_ref[i]
    start = total[:TILE].astype(BF16).astype(F32)
    total = jnp.concatenate([start, total[:TILE] - start, total[TILE:]], axis=0).astype(BF16)
    for i in range(out_ref.shape[0]):
        out_ref[i] = total


def split(arrived, count):
    return pl.pallas_call(
        split_kernel,
        out_shape=shape((count, arrived.shape[1] + TILE, LANES), BF16),
        compiler_params=params(),
        name="split",
    )(arrived)


def inverse_of(core, eye):
    diagonal = 1.0 / jnp.sum(core * eye, axis=0, keepdims=True)
    size = jnp.max(jnp.sum(jnp.abs(core), axis=0))
    spread = jnp.max(jnp.sum(jnp.abs(eye - core * diagonal), axis=0))
    scale = jnp.where(spread < 0.9, diagonal, 2.0 / (1.0 + size))

    def keep_going(state):
        step, _, rest = state
        return jnp.logical_and(step < 48, jnp.max(jnp.abs(rest)) > 1e-6)

    def improve(state):
        step, value, rest = state
        value = value + exact_dot(value, rest)
        return step + 1, value, eye - exact_dot(core, value)

    return lax.while_loop(keep_going, improve, (0, eye * scale, eye - core * scale))[1]


def last_kernel(arrived_ref, *refs):
    basis_refs, (solution_ref, coefficients_ref, total) = refs[:LEVELS], refs[LEVELS:]
    rank = total.shape[1]
    columns = total.shape[2] - rank
    for chunk in range(arrived_ref.shape[0]):
        rows, lanes = place_of(chunk, rank)
        for j in range(0, LEVELS + 1, 2):
            both = arrived_ref[chunk, j * TILE : (j + 2) * TILE, :].astype(F32)
            if j == 0:
                total[0, rows, lanes] = both[:TILE] + both[TILE:]
            else:
                total[j - 1, rows, lanes] = both[:TILE]
                total[j, rows, lanes] = both[TILE:]
    eye = (
        lax.broadcasted_iota(jnp.int32, (rank, rank), 0) == lax.broadcasted_iota(jnp.int32, (rank, rank), 1)
    ).astype(F32)
    core_inverse = parts(inverse_of(eye + total[0, :, columns:], eye))
    change = [None] + [parts(dot3(core_inverse, parts(total[j, :, columns:]))) for j in range(1, LEVELS)]
    right = total[0, :, :columns]
    plain = [dot3(core_inverse, parts(right))]
    for k in range(1, LEVELS):
        right += total[k, :, :columns]
        plain.append(dot3(core_inverse, parts(right)))
    found, halves = [], []
    for k in range(LEVELS):
        value = plain[k]
        for j in range(k, 0, -1):
            value -= dot3(change[j], halves[k - j])
        found.append(value)
        halves.append(parts(value))
    coefficients_ref[...] = found[-1]
    solution = basis_refs[-1][:, :columns]
    for k in range(LEVELS):
        weight = found[ITERS - k]
        if k < ITERS:
            weight = weight - found[ITERS - k - 1]
        solution -= dot3(parts(basis_refs[k][:, columns:]), parts(weight))
    solution_ref[...] = solution


def last_step(arrived, bases, rank):
    rows, width = bases[0].shape
    return pl.pallas_call(
        last_kernel,
        out_shape=(shape((rows, width - rank)), shape((rank, width - rank))),
        scratch_shapes=[pltpu.VMEM((LEVELS, rank, width), F32)],
        compiler_params=params(),
        name="last_step",
    )(arrived, *bases)


def exchanged(array, axes):
    return lax.all_to_all(array, axes, 0, 0, tiled=True)


def on_device(sources, ordering, inverse, low_rank, nearby_blocks, near_index):
    leaves = inverse.shape[0]
    count = lax.axis_size(AXES)
    position = lax.axis_index(AXES)
    even = position % 2 == 0
    offset = near_index - position * leaves
    after = 2 * leaves
    targets = jnp.where(
        offset < 0,
        offset + leaves + jnp.where(even, after, 0),
        jnp.where(offset < leaves, offset + leaves, offset - leaves + jnp.where(even, 0, after)),
    )
    within = [(i, i ^ 1) for i in range(count)]
    across = [(i, j) for i in range(1, count - 1) for j in (i + 1 if i % 2 else i - 1,)]
    basis, sent, inverse_high, inverse_low, near = first_step(
        ordering.reshape(1, -1), sources, inverse, low_rank, nearby_blocks
    )
    plane, line = lax.axis_size(PLANE), lax.axis_size(LINE)
    bases, sums = [basis], []
    own = to_pair = to_cross = sent
    for k in range(ITERS):
        cross = lax.ppermute(to_cross, AXES, across)
        pair = lax.ppermute(to_pair, AXES, within)
        if k == ITERS - 1:
            break
        extras = ()
        if k == 0:
            high, low, after, back_own, *extras = turned(targets, low_rank, basis, near)
        else:
            after = projected(high, low, bases[-1])
        if k == 1:
            back = (back_own, pair, cross)
        sums.append(after)
        value, *sent = sweep(
            targets, own, pair, cross, near, inverse_high, inverse_low, basis, after, extras, 1 if k else 2
        )
        bases.append(value)
        own = to_pair = sent[0]
        to_cross = sent[-1]
    arrived = exchanged(packed(high, low, bases[-1], own, back, sums, plane), PLANE)
    value, after = last_sweep(arrived, line, targets, own, pair, cross, near, inverse_high, inverse_low, basis)
    bases.append(value)
    arrived = exchanged(after, LINE)
    arrived = exchanged(split(arrived, plane), PLANE)
    return last_step(arrived, bases, low_rank.shape[1])


def solution(mesh):
    torus = Mesh(mesh.devices.reshape(8, 4, 4, 2), AXES)
    placed = (
        P(AXES, None),
        P(AXES),
        P(AXES, None, None),
        P(AXES, None),
        P(AXES, None, None, None),
        P(AXES, None),
    )
    return jax.shard_map(
        on_device, mesh=torus, in_specs=placed, out_specs=(P(AXES, None), P()), check_vma=False
    )
```

```python
import functools

import jax
import jax.numpy as jnp
from jax import lax
from jax.experimental import pallas as pl
from jax.experimental.pallas import tpu as pltpu
from jax.sharding import Mesh
from jax.sharding import PartitionSpec as P

ITERS = 4
LEVELS = ITERS + 1
AXES = ("leaf_0", "leaf_1", "sib_0", "sib_1")
PLANE = ("leaf_1", "sib_0", "sib_1")
LINE = "leaf_0"
F32 = jnp.float32
BF16 = jnp.bfloat16
VMEM_LIMIT = 16 * 1024 * 1024
VMEM = pl.BlockSpec(memory_space=pltpu.VMEM)
ANY = pl.BlockSpec(memory_space=pl.ANY)
HBM = pl.BlockSpec(memory_space=pltpu.HBM)
SMEM = pl.BlockSpec(memory_space=pltpu.SMEM)
TILE = 8
LANES = 128


def params():
    return pltpu.CompilerParams(vmem_limit_bytes=VMEM_LIMIT)


def dot(a, b):
    return jnp.dot(a, b, preferred_element_type=F32)


def dot_rows(a, b):
    return lax.dot_general(a, b, (((0,), (0,)), ((), ())), preferred_element_type=F32)


def exact_dot(a, b):
    return jnp.dot(a, b, preferred_element_type=F32, precision=lax.Precision.HIGHEST)


def parts(value):
    high = value.astype(BF16)
    return high, (value - high.astype(F32)).astype(BF16)


def dot3(a, b):
    (a_high, a_low), (b_high, b_low) = a, b
    return dot(a_high, b_high) + (dot(a_high, b_low) + dot(a_low, b_high))


def shape(dims, dtype=F32):
    return jax.ShapeDtypeStruct(dims, dtype)


def first_kernel(
    order_hbm, source_hbm, inverse_hbm, factor_hbm, near_hbm,
    basis_ref, sent_ref, high_ref, low_ref, near_ref, order_ref, source, factor, inverse, sems,
):
    leaves, size, _ = inverse.shape
    columns = source.shape[1]
    pairs = (
        (order_hbm, order_ref),
        (source_hbm, source),
        (factor_hbm, factor),
        (inverse_hbm, inverse),
        (near_hbm, near_ref),
    )
    copies = [pltpu.make_async_copy(a, b, sems.at[i]) for i, (a, b) in enumerate(pairs)]
    for copy in copies:
        copy.start()
    row = lax.broadcasted_iota(jnp.int32, (size, size), 0)
    copies[0].wait()
    copies[1].wait()
    ordered = []
    for leaf in range(leaves):
        here = pl.ds(leaf * size, size)
        order = order_ref[:, leaf * size : (leaf + 1) * size] & (size - 1)
        chosen = (row == order).astype(F32).astype(BF16)
        ordered.append(dot_rows(chosen, jnp.concatenate(parts(source[here, :]), axis=1)).astype(BF16))
    copies[2].wait()
    copies[3].wait()
    for leaf in range(leaves):
        here = pl.ds(leaf * size, size)
        factor_high, factor_low = parts(factor[here, :])
        inverse_high, inverse_low = parts(inverse[leaf])
        high_ref[leaf] = inverse_high
        low_ref[leaf] = inverse_low
        high = jnp.concatenate([ordered[leaf][:, :columns], factor_high], axis=1)
        low = jnp.concatenate([ordered[leaf][:, columns:], factor_low], axis=1)
        basis = dot3((inverse_high, inverse_low), (high, low))
        basis_ref[here, :] = basis
        sent_ref[here, :] = basis.astype(BF16)
    copies[4].wait()


def first_step(order, sources, inverse, factor, near):
    rows, columns = sources.shape
    width = columns + factor.shape[1]
    return pl.pallas_call(
        first_kernel,
        out_shape=(
            shape((rows, width)),
            shape((rows, width), BF16),
            shape(inverse.shape, BF16),
            shape(inverse.shape, BF16),
            shape(near.shape, BF16),
        ),
        in_specs=[HBM] * 5,
        out_specs=(VMEM,) * 5,
        scratch_shapes=[
            pltpu.VMEM(order.shape, jnp.int32),
            pltpu.VMEM(sources.shape, F32),
            pltpu.VMEM(factor.shape, F32),
            pltpu.VMEM(inverse.shape, F32),
            pltpu.SemaphoreType.DMA((5,)),
        ],
        compiler_params=params(),
        name="first_step",
    )(*(pltpu.with_memory_space_constraint(v, pltpu.HBM) for v in (order, sources, inverse, factor, near)))


def turn_kernel(
    target_ref, factor_ref, basis_ref, near_ref,
    high_ref, low_ref, sum_ref, own_ref, pair_ref, cross_ref, total,
):
    leaves, near, size, _ = near_ref.shape
    columns = basis_ref.shape[1] - factor_ref.shape[1]
    rank = factor_ref.shape[1]
    factor_high, factor_low = parts(factor_ref[...])
    high_ref[...] = factor_high.T
    low_ref[...] = factor_low.T
    sum_ref[...] = dot3((high_ref[...], low_ref[...]), parts(basis_ref[...]))
    total[...] = jnp.zeros_like(total)
    for leaf in range(leaves):
        lifted = basis_ref[leaf * size : (leaf + 1) * size, columns:].astype(BF16).T
        for k in range(near):
            total[target_ref[leaf, k]] += dot(lifted, near_ref[leaf, k])
    for leaf in range(leaves):
        here = slice(leaf * rank, (leaf + 1) * rank)
        pair_ref[here, :] = total[leaf].astype(BF16)
        own_ref[here, :] = total[leaves + leaf]
        cross_ref[here, :] = total[2 * leaves + leaf].astype(BF16)


def turned(targets, factor, basis, near):
    rows, rank = factor.shape
    leaves, size = near.shape[0], near.shape[2]
    back = (leaves * rank, size)
    return pl.pallas_call(
        turn_kernel,
        out_shape=(
            shape((rank, rows), BF16),
            shape((rank, rows), BF16),
            shape((rank, basis.shape[1])),
            shape(back),
            shape(back, BF16),
            shape(back, BF16),
        ),
        in_specs=[SMEM] + [VMEM] * 3,
        out_specs=(VMEM,) * 6,
        scratch_shapes=[pltpu.VMEM((3 * leaves, rank, size), F32)],
        compiler_params=params(),
        name="turned",
    )(targets, factor, basis, near)


def project_kernel(high_ref, low_ref, value_ref, sum_ref):
    sum_ref[...] = dot3((high_ref[...], low_ref[...]), parts(value_ref[...]))


def projected(high, low, value):
    return pl.pallas_call(
        project_kernel,
        out_shape=shape((high.shape[0], value.shape[1])),
        compiler_params=params(),
        name="projected",
    )(high, low, value)


def add_kernel(in_ref, out_ref):
    total = in_ref[0].astype(F32)
    for i in range(1, in_ref.shape[0]):
        total += in_ref[i].astype(F32)
    out_ref[...] = jnp.concatenate([total[:TILE] + total[TILE : 2 * TILE], total[2 * TILE :]], axis=0)


def added(arrived):
    return pl.pallas_call(
        add_kernel,
        out_shape=shape((arrived.shape[1] - TILE, LANES)),
        compiler_params=params(),
        name="added",
    )(arrived)


def last_sweep_kernel(line_ref, *refs):
    added_ref, window = refs[-2], refs[-1]
    sweep_kernel(0, *refs[:8], None, refs[8], window)
    for i in range(added_ref.shape[0]):
        added_ref[i] = line_ref[...]


def last_sweep(line, count, targets, own, pair, cross, near, high, low, basis):
    leaves, size = near.shape[0], near.shape[2]
    return pl.pallas_call(
        last_sweep_kernel,
        out_shape=(shape(basis.shape), shape((count, *line.shape))),
        in_specs=[VMEM, SMEM] + [VMEM] * 7,
        out_specs=(VMEM, VMEM),
        scratch_shapes=[pltpu.VMEM((3 * leaves, size, basis.shape[1]), BF16)],
        compiler_params=params(),
        name="last_sweep",
    )(line, targets, own, pair, cross, near, high, low, basis)


def sweep_kernel(extras, target_ref, own_ref, pair_ref, cross_ref, near_ref, high_ref, low_ref, basis_ref, *refs):
    extra_refs, next_ref, sent_refs, window = refs[1 : 1 + extras], refs[1 + extras], refs[2 + extras : -1], refs[-1]
    leaves, near, size, _ = near_ref.shape
    for place, ref in enumerate((pair_ref, own_ref, cross_ref)):
        for leaf in range(leaves):
            window[place * leaves + leaf] = ref[leaf * size : (leaf + 1) * size, :]
    for extra_ref, sent_ref in zip(extra_refs, sent_refs):
        sent_ref[leaves * size :, :] = extra_ref[...]
    for leaf in range(leaves):
        here = pl.ds(leaf * size, size)
        image = dot(near_ref[leaf, 0], window[target_ref[leaf, 0]])
        for k in range(1, near):
            image += dot(near_ref[leaf, k], window[target_ref[leaf, k]])
        value = basis_ref[here, :] - dot3((high_ref[leaf], low_ref[leaf]), parts(image))
        next_ref[here, :] = value
        for sent_ref in sent_refs:
            sent_ref[here, :] = value.astype(BF16)


def sweep(targets, own, pair, cross, near, high, low, basis, after, extras, sends):
    leaves, size = near.shape[0], near.shape[2]
    rows, width = basis.shape
    sent = shape((rows + (extras[0].shape[0] if extras else 0), width), BF16)
    return pl.pallas_call(
        functools.partial(sweep_kernel, len(extras)),
        out_shape=(shape(basis.shape),) + (sent,) * sends,
        in_specs=[SMEM] + [VMEM] * 7 + [ANY] + [VMEM] * len(extras),
        out_specs=(VMEM,) * (1 + sends),
        scratch_shapes=[pltpu.VMEM((3 * leaves, size, width), BF16)],
        compiler_params=params(),
        name="sweep",
    )(targets, own, pair, cross, near, high, low, basis, after, *extras)


def place_of(chunk, rank):
    half, rest = divmod(chunk * TILE, rank)
    return slice(rest, rest + TILE), slice(half * LANES, half * LANES + LANES)


def pack_kernel(high_ref, low_ref, value_ref, sent_ref, own_ref, pair_ref, cross_ref, *refs):
    sum_refs, (out_ref, changes) = refs[: ITERS - 1], refs[ITERS - 1 :]
    rank = changes.shape[1]
    size = own_ref.shape[1]
    leaves = own_ref.shape[0] // rank
    sums = [ref[...] for ref in sum_refs]
    sums.append(dot3((high_ref[...], low_ref[...]), parts(value_ref[...])))
    final = sums[0]
    for leaf in range(leaves):
        here = slice(leaf * rank, (leaf + 1) * rank)
        there = slice(leaves * size + leaf * rank, leaves * size + (leaf + 1) * rank)
        back_high, back_low = parts(own_ref[here, :] + pair_ref[there, :].astype(F32) + cross_ref[there, :].astype(F32))
        sent = sent_ref[leaf * size : (leaf + 1) * size, :]
        final -= dot(back_high, sent) + dot(back_low, sent)
    sums.append(final)
    start = sums[0].astype(BF16).astype(F32)
    changes[0] = start
    changes[1] = sums[0] - start
    for j in range(1, LEVELS):
        changes[j + 1] = sums[j] - sums[j - 1]
    for chunk in range(out_ref.shape[0]):
        rows, lanes = place_of(chunk, rank)
        for j in range(0, LEVELS + 1, 2):
            both = jnp.concatenate([changes[j, rows, lanes], changes[j + 1, rows, lanes]], axis=0)
            out_ref[chunk, j * TILE : (j + 2) * TILE, :] = both.astype(BF16)


def packed(high, low, value, sent, back, sums, count):
    rank, width = sums[0].shape
    return pl.pallas_call(
        pack_kernel,
        out_shape=shape((count, (LEVELS + 1) * TILE, LANES), BF16),
        scratch_shapes=[pltpu.VMEM((LEVELS + 1, rank, width), F32)],
        compiler_params=params(),
        name="packed",
    )(high, low, value, sent, *back, *sums)


def split_kernel(in_ref, out_ref):
    total = in_ref[0]
    for i in range(1, in_ref.shape[0]):
        total += in_ref[i]
    start = total[:TILE].astype(BF16).astype(F32)
    total = jnp.concatenate([start, total[:TILE] - start, total[TILE:]], axis=0).astype(BF16)
    for i in range(out_ref.shape[0]):
        out_ref[i] = total


def split(arrived, count):
    return pl.pallas_call(
        split_kernel,
        out_shape=shape((count, arrived.shape[1] + TILE, LANES), BF16),
        compiler_params=params(),
        name="split",
    )(arrived)


def inverse_of(core, eye):
    diagonal = 1.0 / jnp.sum(core * eye, axis=0, keepdims=True)
    size = jnp.max(jnp.sum(jnp.abs(core), axis=0))
    spread = jnp.max(jnp.sum(jnp.abs(eye - core * diagonal), axis=0))
    scale = jnp.where(spread < 0.9, diagonal, 2.0 / (1.0 + size))

    def keep_going(state):
        step, _, rest = state
        return jnp.logical_and(step < 48, jnp.max(jnp.abs(rest)) > 1e-6)

    def improve(state):
        step, value, rest = state
        value = value + exact_dot(value, rest)
        return step + 1, value, eye - exact_dot(core, value)

    return lax.while_loop(keep_going, improve, (0, eye * scale, eye - core * scale))[1]


def last_kernel(arrived_ref, *refs):
    basis_refs, (solution_ref, coefficients_ref, total) = refs[:LEVELS], refs[LEVELS:]
    rank = total.shape[1]
    columns = total.shape[2] - rank
    for chunk in range(arrived_ref.shape[0]):
        rows, lanes = place_of(chunk, rank)
        for j in range(0, LEVELS + 1, 2):
            both = arrived_ref[chunk, j * TILE : (j + 2) * TILE, :].astype(F32)
            if j == 0:
                total[0, rows, lanes] = both[:TILE] + both[TILE:]
            else:
                total[j - 1, rows, lanes] = both[:TILE]
                total[j, rows, lanes] = both[TILE:]
    eye = (
        lax.broadcasted_iota(jnp.int32, (rank, rank), 0) == lax.broadcasted_iota(jnp.int32, (rank, rank), 1)
    ).astype(F32)
    core_inverse = parts(inverse_of(eye + total[0, :, columns:], eye))
    change = [None] + [parts(dot3(core_inverse, parts(total[j, :, columns:]))) for j in range(1, LEVELS)]
    right = total[0, :, :columns]
    plain = [dot3(core_inverse, parts(right))]
    for k in range(1, LEVELS):
        right += total[k, :, :columns]
        plain.append(dot3(core_inverse, parts(right)))
    found, halves = [], []
    for k in range(LEVELS):
        value = plain[k]
        for j in range(k, 0, -1):
            value -= dot3(change[j], halves[k - j])
        found.append(value)
        halves.append(parts(value))
    coefficients_ref[...] = found[-1]
    solution = basis_refs[-1][:, :columns]
    for k in range(LEVELS):
        weight = found[ITERS - k]
        if k < ITERS:
            weight = weight - found[ITERS - k - 1]
        solution -= dot3(parts(basis_refs[k][:, columns:]), parts(weight))
    solution_ref[...] = solution


def last_step(arrived, bases, rank):
    rows, width = bases[0].shape
    return pl.pallas_call(
        last_kernel,
        out_shape=(shape((rows, width - rank)), shape((rank, width - rank))),
        scratch_shapes=[pltpu.VMEM((LEVELS, rank, width), F32)],
        compiler_params=params(),
        name="last_step",
    )(arrived, *bases)


def exchanged(array, axes):
    return lax.all_to_all(array, axes, 0, 0, tiled=True)


def on_device(sources, ordering, inverse, low_rank, nearby_blocks, near_index):
    leaves = inverse.shape[0]
    count = lax.axis_size(AXES)
    position = lax.axis_index(AXES)
    even = position % 2 == 0
    offset = near_index - position * leaves
    after = 2 * leaves
    targets = jnp.where(
        offset < 0,
        offset + leaves + jnp.where(even, after, 0),
        jnp.where(offset < leaves, offset + leaves, offset - leaves + jnp.where(even, 0, after)),
    )
    within = [(i, i ^ 1) for i in range(count)]
    across = [(i, j) for i in range(1, count - 1) for j in (i + 1 if i % 2 else i - 1,)]
    basis, sent, inverse_high, inverse_low, near = first_step(
        ordering.reshape(1, -1), sources, inverse, low_rank, nearby_blocks
    )
    plane, line = lax.axis_size(PLANE), lax.axis_size(LINE)
    bases, sums = [basis], []
    own = to_pair = to_cross = sent
    for k in range(ITERS):
        cross = lax.ppermute(to_cross, AXES, across)
        pair = lax.ppermute(to_pair, AXES, within)
        if k == ITERS - 1:
            break
        extras = ()
        if k == 0:
            high, low, after, back_own, *extras = turned(targets, low_rank, basis, near)
        else:
            after = projected(high, low, bases[-1])
        if k == 1:
            back = (back_own, pair, cross)
        sums.append(after)
        value, *sent = sweep(
            targets, own, pair, cross, near, inverse_high, inverse_low, basis, after, extras, 1 if k else 2
        )
        bases.append(value)
        own = to_pair = sent[0]
        to_cross = sent[-1]
    lines = packed(high, low, bases[-1], own, back, sums, plane)
    arrived = exchanged(lines, PLANE)
    value, after = last_sweep(added(arrived), line, targets, own, pair, cross, near, inverse_high, inverse_low, basis)
    bases.append(value)
    arrived = exchanged(after, LINE)
    arrived = exchanged(split(arrived, plane), PLANE)
    return last_step(arrived, bases, low_rank.shape[1])


def solution(mesh):
    torus = Mesh(mesh.devices.reshape(8, 4, 4, 2), AXES)
    placed = (
        P(AXES, None),
        P(AXES),
        P(AXES, None, None),
        P(AXES, None),
        P(AXES, None, None, None),
        P(AXES, None),
    )
    return jax.shard_map(
        on_device, mesh=torus, in_specs=placed, out_specs=(P(AXES, None), P()), check_vma=False
    )
```
